32 devices in a mesh: child: 4 (over y, x), row: 4 (over z), col: 2 (over core).
Axes of the slice: x: 2, y: 2, z: 4, core: 2. Of those that a mesh axis runs over, the one named last changes fastest.
Arguments:
- parent_solution: float32 [4096, 256], P(('child', 'row', 'col')), may hold values from -6 to 6
- border_owner: int32 [4, 2048, 1], replicated, may hold values from 0 to 31; in each aligned block of 256 rows (0 to 255, 256 to 511, ..., all dimensions but the last counted through in order) at most 16 rows name the same one
- border_slot: int32 [4, 2048], replicated, may hold values from 0 to 127
- border_tile: float32 [4, 2048, 8192], P('child', 'row', 'col'), may hold values from -0.125 to 0.125
- pivot_inverse: float32 [4, 8192, 8192], P('child', 'row', 'col'), may hold values from -0.0625 to 0.0625
- pivot_rhs: float32 [4, 8192, 256], P('child', 'col'), may hold values from -6 to 6
Outputs:
- pivot_solution: float32 [4, 8192, 256], P('child', ('row', 'col'))
The draws below stay inside these ranges and needn't reach their ends.
Inputs may be any that keep to these rules, and one draw needn't show every extreme that they name: `border_owner`: within each aligned block of 256 border rows of one front, no device is named more than 16 times, and some device is named exactly 16 times in some blocks.
All inputs are finite; a program needn't handle non-finite values.
Results may differ from the reference program's by a relative error of at most 0.0003.
Values sent between devices are 32-bit elements; how exact they have to be, the bound alone decides.
A program may use at most 128 MiB of HBM per device.

```python
import math
import jax
import jax.numpy as jnp
import numpy as np
from jax import lax

BD = 256
P_SIZE = 8192
LOADS = 256
NPD = 128
B = 2048
NPAR = 4096
CAP = 16
N_CHILD = 4
DEVICES = 32


def place_ends(array, rng, least, largest):
    index_at = [jax.random.randint(jax.random.fold_in(rng, axis), (), 0, length) for axis, length in enumerate(array.shape)]
    widest = array.shape.index(max(array.shape))
    next_to = index_at[:widest] + [(index_at[widest] + 1) % array.shape[widest]] + index_at[widest + 1:]
    return array.at[tuple(index_at)].set(least).at[tuple(next_to)].set(largest)


def block_scale(rng, extent, split, least, largest):
    def one(axis_at, parts):
        heights = jax.random.uniform(jax.random.fold_in(jax.random.fold_in(rng, 6), axis_at), (parts,), jnp.float32, least / len(split), largest / len(split))
        return jnp.repeat(jnp.exp(heights), extent[axis_at] // parts).reshape((-1,) + (1,) * (len(extent) - axis_at - 1))

    level = one(*split[0])
    for cut in split[1:]:
        level = level * one(*cut)
    return level


def deal_out(rng, own, number, rows, count, top, limit, slope):
    order = jax.random.permutation(rng, count)
    crowded, ordinary = load_shares(count, rows * top, limit, slope, True), load_shares(count, rows * top, limit, slope, False)
    places = jnp.arange(count)

    def named(lengths, turn):
        used = int((lengths > 0).sum())
        fixed = max(1, used // 4)
        shifted = fixed + (places - fixed + turn * (used - fixed)) % max(1, count - fixed)
        return jnp.zeros((count,), jnp.int32).at[order[jnp.where(places < fixed, places, shifted)]].set(jnp.asarray(lengths, jnp.int32))

    lengths = jnp.where(number % 4 == 0, named(crowded, number // 4), named(ordinary, number - number // 4 - 1))
    mixed = jax.random.permutation(jax.random.fold_in(own, 3), count)
    source_of, sink = mixed[0:count // 2 * 2:2], mixed[1:count // 2 * 2:2]
    margin = jnp.minimum(lengths[source_of] - 1, limit - lengths[sink]) // 2
    margin = jnp.where((source_of == order[0]) | (sink == order[0]) | (lengths[sink] == 0), 0, jnp.maximum(margin, 0))
    shifted = jax.random.randint(jax.random.fold_in(own, 4), (count // 2,), 0, 1 << 20) % (margin + 1)
    lengths = lengths.at[source_of].add(-shifted).at[sink].add(shifted)
    labels = jnp.searchsorted(jnp.cumsum(lengths), jnp.arange(rows * top), side="right").astype(jnp.int32)
    listing = labels.reshape(top, rows).T
    listing = listing[jax.random.permutation(jax.random.fold_in(own, 1), rows)]
    turn = jax.random.randint(jax.random.fold_in(own, 2), (rows, 1), 0, top)
    return jnp.take_along_axis(listing, (jnp.arange(top)[None, :] + turn) % top, axis=1)


def load_shares(amount, total, bound, slope, full):
    loads = [(1 << 20) // math.isqrt(grade ** slope) + 1 for grade in range(1, amount + 1)]
    largest = bound if full else min(bound, max(-(-total // amount), total * loads[0] // sum(loads)))
    least = 1 if total - largest >= amount - 1 else 0
    given, rest = [largest] + [least] * (amount - 1), total - largest - least * (amount - 1)
    while rest > 0:
        movable = [i for i in range(1, amount) if given[i] < largest] or [i for i in range(1, amount) if given[i] < bound]
        pool, remaining = sum([loads[i] for i in movable]), rest
        for i in movable:
            addition = min(bound - given[i], max(1, remaining * loads[i] // pool), rest)
            given[i] = given[i] + addition
            rest = rest - addition
    return np.array(given)


def normal_values(stream_key, shape, width, reach, split=(), dtype=jnp.bfloat16):
    entries = jax.random.normal(stream_key, shape, jnp.float32) * width
    if len(split) > 0:
        entries = block_scale(stream_key, shape, split, -0.22, 0.18) * entries
    return jnp.clip(entries, min=-reach, max=reach).astype(dtype)


def setup_inputs(seed: int = 0) -> dict:
    streams_of = jax.random.split(jax.random.key(seed), 7)
    parent_solution = normal_values(streams_of[0], (NPAR, LOADS), 1.0, 6.0, ((0, 32),), jnp.float32)
    border_owner_keys = jax.random.split(jax.random.fold_in(streams_of[1], 1), N_CHILD * B // BD)
    border_owner_turns = jax.random.permutation(jax.random.fold_in(streams_of[1], 3), N_CHILD * B // BD)
    border_owner = jax.vmap(lambda own, number: deal_out(jax.random.fold_in(streams_of[1], 2), own, number, BD, DEVICES, 1, CAP, 2))(border_owner_keys, border_owner_turns).reshape((N_CHILD, B, 1))
    border_slot = place_ends(jax.random.randint(streams_of[2], (N_CHILD, B), 0, NPD), jax.random.fold_in(streams_of[2], 1), 0, NPD - 1).astype(jnp.int32)
    border_tile = normal_values(streams_of[3], (N_CHILD, B, P_SIZE), B ** -0.5, 0.125, ((0, 4), (1, 4), (2, 2)), jnp.float32)
    pivot_inverse = normal_values(streams_of[4], (N_CHILD, P_SIZE, P_SIZE), P_SIZE ** -0.5, 0.0625, ((0, 4), (1, 4), (2, 2)), jnp.float32)
    pivot_rhs = normal_values(streams_of[5], (N_CHILD, P_SIZE, LOADS), 1.0, 6.0, ((0, 4), (1, 2)), jnp.float32)
    return dict(parent_solution=parent_solution, border_owner=border_owner, border_slot=border_slot, border_tile=border_tile, pivot_inverse=pivot_inverse, pivot_rhs=pivot_rhs)


def reference(parent_solution, border_owner, border_slot, border_tile, pivot_inverse, pivot_rhs):
    parent_index = (border_owner[:, :, 0] * NPD + border_slot).astype(jnp.int32)
    results = []
    for front_number in range(N_CHILD):
        border_values = jnp.take(parent_solution, parent_index[front_number], axis=0)
        coupled = jnp.dot(border_tile[front_number].T, border_values, precision=lax.Precision.HIGHEST, preferred_element_type=jnp.float32)
        reduced = pivot_rhs[front_number] - coupled
        solved = jnp.dot(pivot_inverse[front_number], reduced, precision=lax.Precision.HIGHEST, preferred_element_type=jnp.float32)
        results.append(solved)
    return jnp.stack(results)
```

```python
import functools
import jax
import jax.numpy as jnp
from jax import lax
from jax.experimental import pallas as pl
from jax.experimental.pallas import tpu as pltpu
from jax.sharding import PartitionSpec as P

PIECE = 128
SLOTS = 4
SLACK = 3
bf16, f32 = jnp.bfloat16, jnp.float32


def split2(x):
    hi = x.astype(bf16)
    return hi, (x - hi.astype(f32)).astype(bf16)


def front_kernel(n_row, n_col, bv_ref, tile_ref, inv_ref, rhs_ref, out_ref,
                 bv_all, b_hi, b_lo, tbuf, ibuf, rhs, part, up_s, up_r, dn_s, dn_r, red, acc,
                 tile_sem, inv_sem, rhs_sem, bv_send, bv_recv, us_sem, ur_sem, ds_sem, dr_sem,
                 c_send, c_recv, own_sem):
    row = lax.axis_index("row")
    col = lax.axis_index("col")
    last = n_row - 1
    n_sub = part.shape[0]
    block = bv_ref.shape[0]
    out_rows = acc.shape[0] // n_col
    lead = n_row + SLACK - 1
    rb = min(512, out_rows)
    n_rb = acc.shape[0] // rb
    per = out_rows // rb

    def tile_copy(j):
        return pltpu.make_async_copy(
            tile_ref.at[:, pl.ds(pl.multiple_of(j * PIECE, PIECE), PIECE)], tbuf.at[j], tile_sem.at[j])

    def inv_copy(j):
        slot = lax.rem(j, SLOTS)
        return pltpu.make_async_copy(
            inv_ref.at[:, pl.ds(pl.multiple_of(j * PIECE, PIECE), PIECE)], ibuf.at[slot], inv_sem.at[slot])

    rhs_copy = pltpu.make_async_copy(rhs_ref, rhs, rhs_sem)

    def up_copy(j):
        return pltpu.make_async_remote_copy(
            src_ref=up_s.at[j], dst_ref=up_r.at[j], send_sem=us_sem.at[j], recv_sem=ur_sem.at[j],
            device_id={"row": row + 1}, device_id_type=pl.DeviceIdType.MESH)

    def dn_copy(j):
        return pltpu.make_async_remote_copy(
            src_ref=dn_s.at[j], dst_ref=dn_r.at[j], send_sem=ds_sem.at[j], recv_sem=dr_sem.at[j],
            device_id={"row": row - 1}, device_id_type=pl.DeviceIdType.MESH)

    def start_tile(j, c):
        tile_copy(j).start()
        return c

    lax.fori_loop(0, n_sub, start_tile, 0)
    rhs_copy.start()
    for j in range(min(SLOTS, n_sub)):
        inv_copy(j).start()

    barrier = pltpu.get_barrier_semaphore()

    @pl.when(row > 0)
    def _():
        pl.semaphore_signal(barrier, inc=1, device_id={"row": row - 1}, device_id_type=pl.DeviceIdType.MESH)

    @pl.when(row < last)
    def _():
        pl.semaphore_signal(barrier, inc=1, device_id={"row": row + 1}, device_id_type=pl.DeviceIdType.MESH)

    for q in range(n_col - 1):
        pl.semaphore_signal(barrier, inc=1, device_id={"col": lax.rem(col + 1 + q, n_col)},
                            device_id_type=pl.DeviceIdType.MESH)
    pl.semaphore_wait(barrier, n_col - 1 + jnp.where(row > 0, 1, 0) + jnp.where(row < last, 1, 0))

    bv_copies = []
    for q in range(n_col - 1):
        copy = pltpu.make_async_remote_copy(
            src_ref=bv_ref, dst_ref=bv_all.at[q], send_sem=bv_send.at[q], recv_sem=bv_recv.at[q],
            device_id={"col": lax.rem(col + 1 + q, n_col)}, device_id_type=pl.DeviceIdType.MESH)
        copy.start()
        bv_copies.append(copy)

    acc[...] = jnp.zeros_like(acc)

    def place(owner, value):
        rows = pl.ds(pl.multiple_of(owner * block, block), block)
        hi, lo = split2(value)
        b_hi[rows, :] = hi
        b_lo[rows, :] = lo

    place(col, bv_ref[...])
    for q in range(n_col - 1):
        bv_copies[q].wait_recv()
        place(lax.rem(col + n_col - 1 - q, n_col), bv_all[q])

    def compute_part(j):
        tile_copy(j).wait()
        hi, lo = split2(tbuf[j])
        dims = (((0,), (0,)), ((), ()))
        out = lax.dot_general(hi, b_hi[...], dims, preferred_element_type=f32)
        out += lax.dot_general(hi, b_lo[...], dims, preferred_element_type=f32)
        out += lax.dot_general(lo, b_hi[...], dims, preferred_element_type=f32)
        part[j] = out

    def stage_up(j):
        @pl.when(row == 0)
        def _():
            up_s[j] = part[j]

        @pl.when(row > 0)
        def _():
            up_copy(j).wait_recv()
            up_s[j] = part[j] + up_r[j]

        @pl.when(row < last)
        def _():
            up_copy(j).start()

    def stage_down(j):
        @pl.when(row < last)
        def _():
            dn_copy(j).wait_recv()

        @pl.when(row == last)
        def _():
            dn_s[j] = part[j]

        @pl.when((row > 0) & (row < last))
        def _():
            dn_s[j] = part[j] + dn_r[j]

        @pl.when(row > 0)
        def _():
            dn_copy(j).start()

    def reduce_piece(j):
        @pl.when(row < last)
        def _():
            red[...] = rhs[pl.ds(pl.multiple_of(j * PIECE, PIECE), PIECE), :] - (up_s[j] + dn_r[j])

        @pl.when(row == last)
        def _():
            red[...] = rhs[pl.ds(pl.multiple_of(j * PIECE, PIECE), PIECE), :] - up_s[j]

        r_hi, r_lo = split2(red[...])
        inv_copy(j).wait()
        return jnp.concatenate([r_hi, r_lo, r_hi], axis=0)

    def add_rows(slot, b, right):
        rows = pl.ds(pl.multiple_of(b * rb, rb), rb)
        hi, lo = split2(ibuf[slot, rows, :])
        left = jnp.concatenate([hi, hi, lo], axis=1)
        acc[rows, :] += jnp.dot(left, right, preferred_element_type=f32)

    def step(s, c):
        @pl.when(s < n_sub)
        def _():
            compute_part(s)

        up_lag = jnp.where(row == last, lead, row)
        dn_lag = jnp.where(row == 0, lead, last - row)
        ju = s - up_lag
        jd = s - dn_lag

        @pl.when((ju >= 0) & (ju < n_sub))
        def _():
            stage_up(ju)

        @pl.when((jd >= 0) & (jd < n_sub))
        def _():
            stage_down(jd)

        @pl.when(s == lead)
        def _():
            rhs_copy.wait()

        jf = s - lead

        @pl.when((jf >= 0) & (jf < n_sub - 1))
        def _():
            slot = lax.rem(jf, SLOTS)
            right = reduce_piece(jf)
            for b in range(n_rb):
                add_rows(slot, b, right)

            @pl.when(jf + SLOTS < n_sub)
            def _():
                inv_copy(jf + SLOTS).start()

        return c

    lax.fori_loop(0, n_sub + lead, step, 0)

    right = reduce_piece(n_sub - 1)
    slot = (n_sub - 1) % SLOTS
    sends = []
    for q in range(n_col):
        owner = lax.rem(col + 1 + q, n_col)
        for i in range(per):
            b = owner * per + i
            add_rows(slot, b, right)
            src = acc.at[pl.ds(pl.multiple_of(b * rb, rb), rb), :]
            dst = out_ref.at[col, pl.ds(i * rb, rb), :]
            if q < n_col - 1:
                copy = pltpu.make_async_remote_copy(
                    src_ref=src, dst_ref=dst, send_sem=c_send.at[q, i], recv_sem=c_recv.at[q, i],
                    device_id={"col": owner}, device_id_type=pl.DeviceIdType.MESH)
            else:
                copy = pltpu.make_async_copy(src, dst, own_sem.at[i])
            copy.start()
            sends.append(copy)
    for copy in bv_copies:
        copy.wait_send()

    def drain(j, c):
        @pl.when(row < last)
        def _():
            up_copy(j).wait_send()

        @pl.when(row > 0)
        def _():
            dn_copy(j).wait_send()

        return c

    lax.fori_loop(0, n_sub, drain, 0)
    for copy in sends:
        copy.wait()


def fronts(block_values, tile, inverse, rhs):
    n_row = lax.axis_size("row")
    n_col = lax.axis_size("col")
    block, loads = block_values.shape
    border, pivots = tile.shape
    rows = inverse.shape[0]
    n_sub = pivots // PIECE
    out_rows = rows // n_col
    per = out_rows // min(512, out_rows)
    dma = pltpu.SemaphoreType.DMA
    stream = pltpu.VMEM((n_sub, PIECE, loads), f32)
    hbm = pl.BlockSpec(memory_space=pl.ANY)
    return pl.pallas_call(
        functools.partial(front_kernel, n_row, n_col),
        out_shape=jax.ShapeDtypeStruct((n_col, out_rows, loads), f32),
        in_specs=[pl.BlockSpec(memory_space=pltpu.VMEM), hbm, hbm, hbm],
        out_specs=hbm,
        scratch_shapes=[
            pltpu.VMEM((max(n_col - 1, 1), block, loads), f32),
            pltpu.VMEM((border, loads), bf16),
            pltpu.VMEM((border, loads), bf16),
            pltpu.VMEM((n_sub, border, PIECE), f32),
            pltpu.VMEM((SLOTS, rows, PIECE), f32),
            pltpu.VMEM((pivots, loads), f32),
            stream, stream, stream, stream, stream,
            pltpu.VMEM((PIECE, loads), f32),
            pltpu.VMEM((rows, loads), f32),
            dma((n_sub,)), dma((SLOTS,)), dma(()),
            dma((n_col,)), dma((n_col,)),
            dma((n_sub,)), dma((n_sub,)), dma((n_sub,)), dma((n_sub,)),
            dma((n_col, per)), dma((n_col, per)), dma((per,)),
        ],
        compiler_params=pltpu.CompilerParams(
            collective_id=0, has_side_effects=True, vmem_limit_bytes=60 * 1024 * 1024),
    )(block_values, tile, inverse, rhs)


def running_count(flags):
    length = flags.shape[1]
    steps = jnp.arange(length, dtype=jnp.int32)
    upper = (steps[:, None] <= steps[None, :]).astype(jnp.bfloat16)
    counted = jnp.dot(flags.astype(jnp.bfloat16), upper, preferred_element_type=jnp.float32)
    return counted.astype(jnp.int32)


def shards(parent_solution, border_owner, border_slot, border_tile, pivot_inverse, pivot_rhs):
    highest = lax.Precision.HIGHEST
    devices = lax.axis_size(("child", "row", "col"))
    my_index = lax.axis_index(("child", "row", "col"))
    n_row = lax.axis_size("row")
    n_col = lax.axis_size("col")
    owners = border_owner[:, :, 0]
    border_rows = owners.shape[1]
    block_rows = border_rows // (n_row * n_col)
    capacity = 2 * ((block_rows + devices - 1) // devices)
    local_rows = parent_solution.shape[0]
    loads = parent_solution.shape[1]
    request_owner = owners.reshape(devices, block_rows)
    request_slot = border_slot.reshape(devices, block_rows)
    matched = (request_owner == my_index).astype(jnp.int32)
    position = running_count(matched) - 1
    places = jnp.arange(capacity, dtype=jnp.int32)
    hit = (matched[:, None, :] == 1) & (position[:, None, :] == places[None, :, None])
    table = jnp.sum(jnp.where(hit, request_slot[:, None, :], 0), axis=2)
    filled = jnp.any(hit, axis=2)
    rows_idx = jnp.arange(local_rows, dtype=jnp.int32)
    selector = ((table[:, :, None] == rows_idx[None, None, :]) & filled[:, :, None]).astype(
        jnp.float32
    )
    picked = jnp.dot(
        selector.reshape(-1, local_rows),
        parent_solution,
        precision=highest,
        preferred_element_type=jnp.float32,
    )
    outgoing = picked.reshape(request_owner.shape[0], capacity, loads)
    received = lax.all_to_all(
        outgoing, ("child", "row", "col"), split_axis=0, concat_axis=0, tiled=True
    )
    my_owners = lax.dynamic_index_in_dim(request_owner, my_index, 0, keepdims=False)
    width = received.shape[1]
    owner_ids = jnp.arange(devices, dtype=jnp.int32)
    flags = (owner_ids[:, None] == my_owners[None, :]).astype(jnp.int32)
    counts = running_count(flags)
    position = jnp.sum(flags * counts, axis=0) - 1
    flat = my_owners * width + position
    choose = (flat[:, None] == jnp.arange(devices * width, dtype=jnp.int32)[None, :]).astype(
        jnp.float32
    )
    block_values = jnp.dot(
        choose,
        received.reshape(devices * width, loads),
        precision=highest,
        preferred_element_type=jnp.float32,
    )
    pieces = fronts(block_values, border_tile[0], pivot_inverse[0], pivot_rhs[0])
    return jnp.sum(pieces, axis=0)[None]


def solution(mesh):
    return jax.shard_map(
        shards,
        mesh=mesh,
        in_specs=(
            P(("child", "row", "col"), None),
            P(),
            P(),
            P("child", "row", "col"),
            P("child", "row", "col"),
            P("child", "col", None),
        ),
        out_specs=P("child", ("row", "col"), None),
        check_vma=False,
    )
```

```python
import functools
import jax
import jax.numpy as jnp
from jax import lax
from jax.experimental import pallas as pl
from jax.experimental.pallas import tpu as pltpu
from jax.sharding import PartitionSpec as P

PIECE = 128
SLOTS = 4
SLACK = 3
SKEW = 2
bf16, f32 = jnp.bfloat16, jnp.float32


def split2(x):
    hi = x.astype(bf16)
    return hi, (x - hi.astype(f32)).astype(bf16)


def front_kernel(n_child, n_row, n_col, sel_ref, parent_ref, choose_ref, tile_ref, inv_ref, rhs_ref, out_ref,
                 picked, received, bv_own, bv_all, b_hi, b_lo, tbuf, ibuf, rhs, part, up_s, up_r, dn_s, dn_r, red, acc,
                 g_send, g_recv, tile_sem, inv_sem, rhs_sem, bv_send, bv_recv, us_sem, ur_sem, ds_sem, dr_sem,
                 c_send, c_recv, own_sem):
    row = lax.axis_index("row")
    col = lax.axis_index("col")
    last = n_row - 1
    n_sub = part.shape[0]
    block = bv_own.shape[0]
    child = lax.axis_index("child")
    devices = n_child * n_row * n_col
    me = (child * n_row + row) * n_col + col
    cap = picked.shape[0] // devices
    out_rows = acc.shape[0] // n_col
    lead = SKEW * last + SLACK
    rb = min(512, out_rows)
    n_rb = acc.shape[0] // rb
    per = out_rows // rb

    def tile_copy(j):
        return pltpu.make_async_copy(
            tile_ref.at[:, pl.ds(pl.multiple_of(j * PIECE, PIECE), PIECE)], tbuf.at[j], tile_sem.at[j])

    def inv_copy(j):
        slot = lax.rem(j, SLOTS)
        return pltpu.make_async_copy(
            inv_ref.at[:, pl.ds(pl.multiple_of(j * PIECE, PIECE), PIECE)], ibuf.at[slot], inv_sem.at[slot])

    rhs_copy = pltpu.make_async_copy(rhs_ref, rhs, rhs_sem)

    def up_copy(j):
        return pltpu.make_async_remote_copy(
            src_ref=up_s.at[j], dst_ref=up_r.at[j], send_sem=us_sem.at[j], recv_sem=ur_sem.at[j],
            device_id={"row": row + 1}, device_id_type=pl.DeviceIdType.MESH)

    def dn_copy(j):
        return pltpu.make_async_remote_copy(
            src_ref=dn_s.at[j], dst_ref=dn_r.at[j], send_sem=ds_sem.at[j], recv_sem=dr_sem.at[j],
            device_id={"row": row - 1}, device_id_type=pl.DeviceIdType.MESH)

    def start_tile(j, c):
        tile_copy(j).start()
        return c

    lax.fori_loop(0, n_sub, start_tile, 0)
    rhs_copy.start()
    for j in range(min(SLOTS, n_sub)):
        inv_copy(j).start()

    barrier = pltpu.get_barrier_semaphore()

    def coords(d):
        t = lax.rem(me + d, devices)
        return (t // (n_row * n_col), lax.rem(t // n_col, n_row), lax.rem(t, n_col))

    def greet(d, c):
        pl.semaphore_signal(barrier, inc=1, device_id=coords(d), device_id_type=pl.DeviceIdType.MESH)
        return c

    lax.fori_loop(1, devices, greet, 0)
    p_hi, p_lo = split2(parent_ref[...])
    picked[...] = (jnp.dot(sel_ref[...], p_hi, preferred_element_type=f32)
                   + jnp.dot(sel_ref[...], p_lo, preferred_element_type=f32))
    pl.semaphore_wait(barrier, devices - 1)

    def give(d):
        t = lax.rem(me + d, devices)
        return pltpu.make_async_remote_copy(
            src_ref=picked.at[pl.ds(pl.multiple_of(t * cap, 8), cap), :],
            dst_ref=received.at[pl.ds(pl.multiple_of(me * cap, 8), cap), :],
            send_sem=g_send.at[d], recv_sem=g_recv.at[d],
            device_id=coords(d), device_id_type=pl.DeviceIdType.MESH)

    def start_give(d, c):
        give(d).start()
        return c

    def end_give(d, c):
        give(d).wait_recv()
        return c

    lax.fori_loop(1, devices, start_give, 0)
    mine = pl.ds(pl.multiple_of(me * cap, 8), cap)
    received[mine, :] = picked[mine, :]
    acc[...] = jnp.zeros_like(acc)
    lax.fori_loop(1, devices, end_give, 0)
    g_hi, g_lo = split2(received[...])
    bv_own[...] = (jnp.dot(choose_ref[...], g_hi, preferred_element_type=f32)
                   + jnp.dot(choose_ref[...], g_lo, preferred_element_type=f32))

    bv_copies = []
    for q in range(n_col - 1):
        copy = pltpu.make_async_remote_copy(
            src_ref=bv_own, dst_ref=bv_all.at[q], send_sem=bv_send.at[q], recv_sem=bv_recv.at[q],
            device_id={"col": lax.rem(col + 1 + q, n_col)}, device_id_type=pl.DeviceIdType.MESH)
        copy.start()
        bv_copies.append(copy)

    def place(owner, value):
        rows = pl.ds(pl.multiple_of(owner * block, block), block)
        hi, lo = split2(value)
        b_hi[rows, :] = hi
        b_lo[rows, :] = lo

    place(col, bv_own[...])
    for q in range(n_col - 1):
        bv_copies[q].wait_recv()
        place(lax.rem(col + n_col - 1 - q, n_col), bv_all[q])

    def compute_part(j):
        tile_copy(j).wait()
        hi, lo = split2(tbuf[j])
        dims = (((0,), (0,)), ((), ()))
        out = lax.dot_general(hi, b_hi[...], dims, preferred_element_type=f32)
        out += lax.dot_general(hi, b_lo[...], dims, preferred_element_type=f32)
        out += lax.dot_general(lo, b_hi[...], dims, preferred_element_type=f32)
        part[j] = out

    def stage_up(j):
        @pl.when(row == 0)
        def _():
            up_s[j] = part[j]

        @pl.when(row > 0)
        def _():
            up_copy(j).wait_recv()
            up_s[j] = part[j] + up_r[j]

        @pl.when(row < last)
        def _():
            up_copy(j).start()

    def stage_down(j):
        @pl.when(row < last)
        def _():
            dn_copy(j).wait_recv()

        @pl.when(row == last)
        def _():
            dn_s[j] = part[j]

        @pl.when((row > 0) & (row < last))
        def _():
            dn_s[j] = part[j] + dn_r[j]

        @pl.when(row > 0)
        def _():
            dn_copy(j).start()

    def reduce_piece(j):
        @pl.when(row < last)
        def _():
            red[...] = rhs[pl.ds(pl.multiple_of(j * PIECE, PIECE), PIECE), :] - (up_s[j] + dn_r[j])

        @pl.when(row == last)
        def _():
            red[...] = rhs[pl.ds(pl.multiple_of(j * PIECE, PIECE), PIECE), :] - up_s[j]

        r_hi, r_lo = split2(red[...])
        inv_copy(j).wait()
        return jnp.concatenate([r_hi, r_lo, r_hi], axis=0)

    def add_rows(slot, b, right):
        rows = pl.ds(pl.multiple_of(b * rb, rb), rb)
        hi, lo = split2(ibuf[slot, rows, :])
        left = jnp.concatenate([hi, hi, lo], axis=1)
        acc[rows, :] += jnp.dot(left, right, preferred_element_type=f32)

    def step(s, c):
        @pl.when(s < n_sub)
        def _():
            compute_part(s)

        up_lag = jnp.where(row == last, lead, SKEW * row)
        dn_lag = jnp.where(row == 0, lead, SKEW * (last - row))
        ju = s - up_lag
        jd = s - dn_lag

        @pl.when((ju >= 0) & (ju < n_sub))
        def _():
            stage_up(ju)

        @pl.when((jd >= 0) & (jd < n_sub))
        def _():
            stage_down(jd)

        @pl.when(s == lead)
        def _():
            rhs_copy.wait()

        jf = s - lead

        @pl.when((jf >= 0) & (jf < n_sub - 1))
        def _():
            slot = lax.rem(jf, SLOTS)
            right = reduce_piece(jf)
            for b in range(n_rb):
                add_rows(slot, b, right)

            @pl.when(jf + SLOTS < n_sub)
            def _():
                inv_copy(jf + SLOTS).start()

        return c

    lax.fori_loop(0, n_sub + lead, step, 0)

    right = reduce_piece(n_sub - 1)
    slot = (n_sub - 1) % SLOTS
    sends = []
    for q in range(n_col):
        owner = lax.rem(col + 1 + q, n_col)
        for i in range(per):
            b = owner * per + i
            add_rows(slot, b, right)
            src = acc.at[pl.ds(pl.multiple_of(b * rb, rb), rb), :]
            dst = out_ref.at[col, pl.ds(i * rb, rb), :]
            if q < n_col - 1:
                copy = pltpu.make_async_remote_copy(
                    src_ref=src, dst_ref=dst, send_sem=c_send.at[q, i], recv_sem=c_recv.at[q, i],
                    device_id={"col": owner}, device_id_type=pl.DeviceIdType.MESH)
            else:
                copy = pltpu.make_async_copy(src, dst, own_sem.at[i])
            copy.start()
            sends.append(copy)
    for copy in bv_copies:
        copy.wait_send()

    def drain(j, c):
        @pl.when(row < last)
        def _():
            up_copy(j).wait_send()

        @pl.when(row > 0)
        def _():
            dn_copy(j).wait_send()

        return c

    lax.fori_loop(0, n_sub, drain, 0)

    def end_send(d, c):
        give(d).wait_send()
        return c

    lax.fori_loop(1, devices, end_send, 0)
    for copy in sends:
        copy.wait()


def fronts(selector, parent, choose, tile, inverse, rhs):
    n_child = lax.axis_size("child")
    n_row = lax.axis_size("row")
    n_col = lax.axis_size("col")
    block, wide = choose.shape
    loads = parent.shape[1]
    devices = n_child * n_row * n_col
    border, pivots = tile.shape
    rows = inverse.shape[0]
    n_sub = pivots // PIECE
    out_rows = rows // n_col
    per = out_rows // min(512, out_rows)
    dma = pltpu.SemaphoreType.DMA
    stream = pltpu.VMEM((n_sub, PIECE, loads), f32)
    hbm = pl.BlockSpec(memory_space=pl.ANY)
    return pl.pallas_call(
        functools.partial(front_kernel, n_child, n_row, n_col),
        out_shape=jax.ShapeDtypeStruct((n_col, out_rows, loads), f32),
        in_specs=[pl.BlockSpec(memory_space=pltpu.VMEM)] * 3 + [hbm] * 3,
        out_specs=hbm,
        scratch_shapes=[
            pltpu.VMEM((wide, loads), f32),
            pltpu.VMEM((wide, loads), f32),
            pltpu.VMEM((block, loads), f32),
            pltpu.VMEM((max(n_col - 1, 1), block, loads), f32),
            pltpu.VMEM((border, loads), bf16),
            pltpu.VMEM((border, loads), bf16),
            pltpu.VMEM((n_sub, border, PIECE), f32),
            pltpu.VMEM((SLOTS, rows, PIECE), f32),
            pltpu.VMEM((pivots, loads), f32),
            stream, stream, stream, stream, stream,
            pltpu.VMEM((PIECE, loads), f32),
            pltpu.VMEM((rows, loads), f32),
            dma((devices,)), dma((devices,)),
            dma((n_sub,)), dma((SLOTS,)), dma(()),
            dma((n_col,)), dma((n_col,)),
            dma((n_sub,)), dma((n_sub,)), dma((n_sub,)), dma((n_sub,)),
            dma((n_col, per)), dma((n_col, per)), dma((per,)),
        ],
        compiler_params=pltpu.CompilerParams(
            collective_id=0, has_side_effects=True, vmem_limit_bytes=60 * 1024 * 1024),
    )(selector, parent, choose, tile, inverse, rhs)


def running_count(flags):
    length = flags.shape[1]
    steps = jnp.arange(length, dtype=jnp.int32)
    upper = (steps[:, None] <= steps[None, :]).astype(jnp.bfloat16)
    counted = jnp.dot(flags.astype(jnp.bfloat16), upper, preferred_element_type=jnp.float32)
    return counted.astype(jnp.int32)


def shards(parent_solution, border_owner, border_slot, border_tile, pivot_inverse, pivot_rhs):
    devices = lax.axis_size(("child", "row", "col"))
    my_index = lax.axis_index(("child", "row", "col"))
    n_row = lax.axis_size("row")
    n_col = lax.axis_size("col")
    owners = border_owner[:, :, 0]
    border_rows = owners.shape[1]
    block_rows = border_rows // (n_row * n_col)
    capacity = -(-2 * ((block_rows + devices - 1) // devices) // 8) * 8
    local_rows = parent_solution.shape[0]
    request_owner = owners.reshape(devices, block_rows)
    request_slot = border_slot.reshape(devices, block_rows)
    matched = (request_owner == my_index).astype(jnp.int32)
    position = running_count(matched) - 1
    places = jnp.arange(capacity, dtype=jnp.int32)
    hit = (matched[:, None, :] == 1) & (position[:, None, :] == places[None, :, None])
    table = jnp.sum(jnp.where(hit, request_slot[:, None, :], 0), axis=2)
    filled = jnp.any(hit, axis=2)
    rows_idx = jnp.arange(local_rows, dtype=jnp.int32)
    selector = ((table[:, :, None] == rows_idx[None, None, :]) & filled[:, :, None]).astype(bf16)
    my_owners = lax.dynamic_index_in_dim(request_owner, my_index, 0, keepdims=False)
    owner_ids = jnp.arange(devices, dtype=jnp.int32)
    flags = (owner_ids[:, None] == my_owners[None, :]).astype(jnp.int32)
    counts = running_count(flags)
    position = jnp.sum(flags * counts, axis=0) - 1
    flat = my_owners * capacity + position
    choose = (flat[:, None] == jnp.arange(devices * capacity, dtype=jnp.int32)[None, :]).astype(bf16)
    pieces = fronts(selector.reshape(-1, local_rows), parent_solution, choose,
                    border_tile[0], pivot_inverse[0], pivot_rhs[0])
    return jnp.sum(pieces, axis=0)[None]


def solution(mesh):
    return jax.shard_map(
        shards,
        mesh=mesh,
        in_specs=(
            P(("child", "row", "col"), None),
            P(),
            P(),
            P("child", "row", "col"),
            P("child", "row", "col"),
            P("child", "col", None),
        ),
        out_specs=P("child", ("row", "col"), None),
        check_vma=False,
    )
```

```python
import functools
import jax
import jax.numpy as jnp
from jax import lax
from jax.experimental import pallas as pl
from jax.experimental.pallas import tpu as pltpu
from jax.sharding import PartitionSpec as P

PIECE = 128
SLOTS = 4
SLACK = 3
SKEW = 2
bf16, f32 = jnp.bfloat16, jnp.float32


def split2(x):
    hi = x.astype(bf16)
    return hi, (x - hi.astype(f32)).astype(bf16)


def front_kernel(n_child, n_row, n_col, sel_ref, parent_ref, choose_ref, tile_ref, inv_ref, rhs_ref, out_ref,
                 picked, slabs, received, bv_own, bv_all, b_hi, b_lo, tbuf, ibuf, rhs, part, up_s, up_r, dn_s, dn_r, red, acc,
                 g_send, g_recv, slab_up, slab_dn, slab_recv, tile_sem, inv_sem, rhs_sem, bv_send, bv_recv, us_sem, ur_sem, ds_sem, dr_sem,
                 c_send, c_recv, own_sem):
    row = lax.axis_index("row")
    col = lax.axis_index("col")
    last = n_row - 1
    n_sub = part.shape[0]
    block = bv_own.shape[0]
    child = lax.axis_index("child")
    plane = n_child * n_col
    my_place = child * n_col + col
    cap = received.shape[0] // (n_row * plane)
    out_rows = acc.shape[0] // n_col
    lead = SKEW * last + SLACK
    rb = min(512, out_rows)
    n_rb = acc.shape[0] // rb
    per = out_rows // rb

    def tile_copy(j):
        return pltpu.make_async_copy(
            tile_ref.at[:, pl.ds(pl.multiple_of(j * PIECE, PIECE), PIECE)], tbuf.at[j], tile_sem.at[j])

    def inv_copy(j):
        slot = lax.rem(j, SLOTS)
        return pltpu.make_async_copy(
            inv_ref.at[:, pl.ds(pl.multiple_of(j * PIECE, PIECE), PIECE)], ibuf.at[slot], inv_sem.at[slot])

    rhs_copy = pltpu.make_async_copy(rhs_ref, rhs, rhs_sem)

    def up_copy(j):
        return pltpu.make_async_remote_copy(
            src_ref=up_s.at[j], dst_ref=up_r.at[j], send_sem=us_sem.at[j], recv_sem=ur_sem.at[j],
            device_id={"row": row + 1}, device_id_type=pl.DeviceIdType.MESH)

    def dn_copy(j):
        return pltpu.make_async_remote_copy(
            src_ref=dn_s.at[j], dst_ref=dn_r.at[j], send_sem=ds_sem.at[j], recv_sem=dr_sem.at[j],
            device_id={"row": row - 1}, device_id_type=pl.DeviceIdType.MESH)

    def start_tile(j, c):
        tile_copy(j).start()
        return c

    lax.fori_loop(0, n_sub, start_tile, 0)
    rhs_copy.start()
    for j in range(min(SLOTS, n_sub)):
        inv_copy(j).start()

    barrier = pltpu.get_barrier_semaphore()

    def peer(d):
        e = lax.rem(my_place + d, plane)
        return e, (e // n_col, row, lax.rem(e, n_col))

    def greet(d, c):
        pl.semaphore_signal(barrier, inc=1, device_id=peer(d)[1], device_id_type=pl.DeviceIdType.MESH)
        return c

    lax.fori_loop(1, plane, greet, 0)

    @pl.when(row > 0)
    def _():
        pl.semaphore_signal(barrier, inc=1, device_id={"row": row - 1}, device_id_type=pl.DeviceIdType.MESH)

    @pl.when(row < last)
    def _():
        pl.semaphore_signal(barrier, inc=1, device_id={"row": row + 1}, device_id_type=pl.DeviceIdType.MESH)

    pl.semaphore_wait(barrier, plane - 1 + jnp.where(row > 0, 1, 0) + jnp.where(row < last, 1, 0))

    def slab_copy(src, r, way, send_sem):
        return pltpu.make_async_remote_copy(
            src_ref=src, dst_ref=slabs.at[r], send_sem=send_sem.at[r], recv_sem=slab_recv.at[r],
            device_id={"row": row + way}, device_id_type=pl.DeviceIdType.MESH)

    def give(r, d):
        e, where = peer(d)
        owner = (child * n_row + r) * n_col + col
        return pltpu.make_async_remote_copy(
            src_ref=picked.at[r, pl.ds(pl.multiple_of(e * cap, 8), cap), :],
            dst_ref=received.at[pl.ds(pl.multiple_of(owner * cap, 8), cap), :],
            send_sem=g_send.at[r * plane + d], recv_sem=g_recv.at[r * plane + d],
            device_id=where, device_id_type=pl.DeviceIdType.MESH)

    def pick(r, slab):
        p_hi, p_lo = split2(slab)
        picked[r] = (jnp.dot(sel_ref[r], p_hi, preferred_element_type=f32)
                     + jnp.dot(sel_ref[r], p_lo, preferred_element_type=f32))

        def start_give(d, c):
            give(r, d).start()
            return c

        lax.fori_loop(1, plane, start_give, 0)
        owner = (child * n_row + r) * n_col + col
        received[pl.ds(pl.multiple_of(owner * cap, 8), cap), :] = (
            picked[r, pl.ds(pl.multiple_of(my_place * cap, 8), cap), :])

    @pl.when(row < last)
    def _():
        slab_copy(parent_ref, row, 1, slab_up).start()

    @pl.when(row > 0)
    def _():
        slab_copy(parent_ref, row, -1, slab_dn).start()

    pick(row, parent_ref[...])
    acc[...] = jnp.zeros_like(acc)
    for far in range(1, n_row):
        low, high = row - far, row + far

        @pl.when(low >= 0)
        def _():
            slab_copy(slabs.at[low], low, 1, slab_up).wait_recv()

            @pl.when(row < last)
            def _():
                slab_copy(slabs.at[low], low, 1, slab_up).start()

        @pl.when(high <= last)
        def _():
            slab_copy(slabs.at[high], high, -1, slab_dn).wait_recv()

            @pl.when(row > 0)
            def _():
                slab_copy(slabs.at[high], high, -1, slab_dn).start()

        @pl.when(low >= 0)
        def _():
            pick(low, slabs[low])

        @pl.when(high <= last)
        def _():
            pick(high, slabs[high])

    def end_give(i, c):
        give(i // (plane - 1), lax.rem(i, plane - 1) + 1).wait_recv()
        return c

    lax.fori_loop(0, n_row * (plane - 1), end_give, 0)
    g_hi, g_lo = split2(received[...])
    bv_own[...] = (jnp.dot(choose_ref[...], g_hi, preferred_element_type=f32)
                   + jnp.dot(choose_ref[...], g_lo, preferred_element_type=f32))

    bv_copies = []
    for q in range(n_col - 1):
        copy = pltpu.make_async_remote_copy(
            src_ref=bv_own, dst_ref=bv_all.at[q], send_sem=bv_send.at[q], recv_sem=bv_recv.at[q],
            device_id={"col": lax.rem(col + 1 + q, n_col)}, device_id_type=pl.DeviceIdType.MESH)
        copy.start()
        bv_copies.append(copy)

    def place(owner, value):
        rows = pl.ds(pl.multiple_of(owner * block, block), block)
        hi, lo = split2(value)
        b_hi[rows, :] = hi
        b_lo[rows, :] = lo

    place(col, bv_own[...])
    for q in range(n_col - 1):
        bv_copies[q].wait_recv()
        place(lax.rem(col + n_col - 1 - q, n_col), bv_all[q])

    def compute_part(j):
        tile_copy(j).wait()
        hi, lo = split2(tbuf[j])
        dims = (((0,), (0,)), ((), ()))
        out = lax.dot_general(hi, b_hi[...], dims, preferred_element_type=f32)
        out += lax.dot_general(hi, b_lo[...], dims, preferred_element_type=f32)
        out += lax.dot_general(lo, b_hi[...], dims, preferred_element_type=f32)
        part[j] = out

    def stage_up(j):
        @pl.when(row == 0)
        def _():
            up_s[j] = part[j]

        @pl.when(row > 0)
        def _():
            up_copy(j).wait_recv()
            up_s[j] = part[j] + up_r[j]

        @pl.when(row < last)
        def _():
            up_copy(j).start()

    def stage_down(j):
        @pl.when(row < last)
        def _():
            dn_copy(j).wait_recv()

        @pl.when(row == last)
        def _():
            dn_s[j] = part[j]

        @pl.when((row > 0) & (row < last))
        def _():
            dn_s[j] = part[j] + dn_r[j]

        @pl.when(row > 0)
        def _():
            dn_copy(j).start()

    def reduce_piece(j):
        @pl.when(row < last)
        def _():
            red[...] = rhs[pl.ds(pl.multiple_of(j * PIECE, PIECE), PIECE), :] - (up_s[j] + dn_r[j])

        @pl.when(row == last)
        def _():
            red[...] = rhs[pl.ds(pl.multiple_of(j * PIECE, PIECE), PIECE), :] - up_s[j]

        r_hi, r_lo = split2(red[...])
        inv_copy(j).wait()
        return jnp.concatenate([r_hi, r_lo, r_hi], axis=0)

    def add_rows(slot, b, right):
        rows = pl.ds(pl.multiple_of(b * rb, rb), rb)
        hi, lo = split2(ibuf[slot, rows, :])
        left = jnp.concatenate([hi, hi, lo], axis=1)
        acc[rows, :] += jnp.dot(left, right, preferred_element_type=f32)

    def step(s, c):
        @pl.when(s < n_sub)
        def _():
            compute_part(s)

        up_lag = jnp.where(row == last, lead, SKEW * row)
        dn_lag = jnp.where(row == 0, lead, SKEW * (last - row))
        ju = s - up_lag
        jd = s - dn_lag

        @pl.when((ju >= 0) & (ju < n_sub))
        def _():
            stage_up(ju)

        @pl.when((jd >= 0) & (jd < n_sub))
        def _():
            stage_down(jd)

        @pl.when(s == lead)
        def _():
            rhs_copy.wait()

        jf = s - lead

        @pl.when((jf >= 0) & (jf < n_sub - 1))
        def _():
            slot = lax.rem(jf, SLOTS)
            right = reduce_piece(jf)
            for b in range(n_rb):
                add_rows(slot, b, right)

            @pl.when(jf + SLOTS < n_sub)
            def _():
                inv_copy(jf + SLOTS).start()

        return c

    lax.fori_loop(0, n_sub + lead, step, 0)

    right = reduce_piece(n_sub - 1)
    slot = (n_sub - 1) % SLOTS
    sends = []
    for q in range(n_col):
        owner = lax.rem(col + 1 + q, n_col)
        for i in range(per):
            b = owner * per + i
            add_rows(slot, b, right)
            src = acc.at[pl.ds(pl.multiple_of(b * rb, rb), rb), :]
            dst = out_ref.at[col, pl.ds(i * rb, rb), :]
            if q < n_col - 1:
                copy = pltpu.make_async_remote_copy(
                    src_ref=src, dst_ref=dst, send_sem=c_send.at[q, i], recv_sem=c_recv.at[q, i],
                    device_id={"col": owner}, device_id_type=pl.DeviceIdType.MESH)
            else:
                copy = pltpu.make_async_copy(src, dst, own_sem.at[i])
            copy.start()
            sends.append(copy)
    for copy in bv_copies:
        copy.wait_send()

    def drain(j, c):
        @pl.when(row < last)
        def _():
            up_copy(j).wait_send()

        @pl.when(row > 0)
        def _():
            dn_copy(j).wait_send()

        return c

    lax.fori_loop(0, n_sub, drain, 0)

    def end_send(i, c):
        give(i // (plane - 1), lax.rem(i, plane - 1) + 1).wait_send()
        return c

    lax.fori_loop(0, n_row * (plane - 1), end_send, 0)
    for r in range(n_row):
        @pl.when((row < last) & (r <= row))
        def _():
            slab_copy(parent_ref, r, 1, slab_up).wait_send()

        @pl.when((row > 0) & (r >= row))
        def _():
            slab_copy(parent_ref, r, -1, slab_dn).wait_send()

    for copy in sends:
        copy.wait()


def fronts(selector, parent, choose, tile, inverse, rhs):
    n_child = lax.axis_size("child")
    n_row = lax.axis_size("row")
    n_col = lax.axis_size("col")
    block, wide = choose.shape
    loads = parent.shape[1]
    devices = n_child * n_row * n_col
    border, pivots = tile.shape
    rows = inverse.shape[0]
    n_sub = pivots // PIECE
    out_rows = rows // n_col
    per = out_rows // min(512, out_rows)
    dma = pltpu.SemaphoreType.DMA
    stream = pltpu.VMEM((n_sub, PIECE, loads), f32)
    hbm = pl.BlockSpec(memory_space=pl.ANY)
    return pl.pallas_call(
        functools.partial(front_kernel, n_child, n_row, n_col),
        out_shape=jax.ShapeDtypeStruct((n_col, out_rows, loads), f32),
        in_specs=[pl.BlockSpec(memory_space=pltpu.VMEM)] * 3 + [hbm] * 3,
        out_specs=hbm,
        scratch_shapes=[
            pltpu.VMEM((n_row, wide // n_row, loads), f32),
            pltpu.VMEM((n_row,) + parent.shape, f32),
            pltpu.VMEM((wide, loads), f32),
            pltpu.VMEM((block, loads), f32),
            pltpu.VMEM((max(n_col - 1, 1), block, loads), f32),
            pltpu.VMEM((border, loads), bf16),
            pltpu.VMEM((border, loads), bf16),
            pltpu.VMEM((n_sub, border, PIECE), f32),
            pltpu.VMEM((SLOTS, rows, PIECE), f32),
            pltpu.VMEM((pivots, loads), f32),
            stream, stream, stream, stream, stream,
            pltpu.VMEM((PIECE, loads), f32),
            pltpu.VMEM((rows, loads), f32),
            dma((devices,)), dma((devices,)), dma((n_row,)), dma((n_row,)), dma((n_row,)),
            dma((n_sub,)), dma((SLOTS,)), dma(()),
            dma((n_col,)), dma((n_col,)),
            dma((n_sub,)), dma((n_sub,)), dma((n_sub,)), dma((n_sub,)),
            dma((n_col, per)), dma((n_col, per)), dma((per,)),
        ],
        compiler_params=pltpu.CompilerParams(
            collective_id=0, has_side_effects=True, vmem_limit_bytes=60 * 1024 * 1024),
    )(selector, parent, choose, tile, inverse, rhs)


def running_count(flags):
    length = flags.shape[1]
    steps = jnp.arange(length, dtype=jnp.int32)
    upper = (steps[:, None] <= steps[None, :]).astype(jnp.bfloat16)
    counted = jnp.dot(flags.astype(jnp.bfloat16), upper, preferred_element_type=jnp.float32)
    return counted.astype(jnp.int32)


def shards(parent_solution, border_owner, border_slot, border_tile, pivot_inverse, pivot_rhs):
    devices = lax.axis_size(("child", "row", "col"))
    my_index = lax.axis_index(("child", "row", "col"))
    n_row = lax.axis_size("row")
    n_col = lax.axis_size("col")
    owners = border_owner[:, :, 0]
    border_rows = owners.shape[1]
    block_rows = border_rows // (n_row * n_col)
    capacity = -(-2 * ((block_rows + devices - 1) // devices) // 8) * 8
    local_rows = parent_solution.shape[0]
    request_owner = owners.reshape(devices, block_rows)
    request_slot = border_slot.reshape(devices, block_rows)
    n_child = lax.axis_size("child")
    plane = n_child * n_col
    my_row = lax.axis_index("row")

    def plane_blocks(blocks):
        grid = blocks.reshape(n_child, n_row, n_col, block_rows)
        return lax.dynamic_index_in_dim(grid, my_row, 1, keepdims=False).reshape(1, plane, block_rows)

    line = (lax.axis_index("child") * n_row + jnp.arange(n_row, dtype=jnp.int32)) * n_col + lax.axis_index("col")
    matched = (plane_blocks(request_owner) == line[:, None, None]).astype(jnp.int32)
    matched = matched.reshape(devices, block_rows)
    plane_slot = jnp.broadcast_to(plane_blocks(request_slot), (n_row, plane, block_rows))
    request_slot = plane_slot.reshape(devices, block_rows)
    position = running_count(matched) - 1
    places = jnp.arange(capacity, dtype=jnp.int32)
    hit = (matched[:, None, :] == 1) & (position[:, None, :] == places[None, :, None])
    table = jnp.sum(jnp.where(hit, request_slot[:, None, :], 0), axis=2)
    filled = jnp.any(hit, axis=2)
    rows_idx = jnp.arange(local_rows, dtype=jnp.int32)
    selector = ((table[:, :, None] == rows_idx[None, None, :]) & filled[:, :, None]).astype(bf16)
    my_owners = lax.dynamic_index_in_dim(request_owner, my_index, 0, keepdims=False)
    owner_ids = jnp.arange(devices, dtype=jnp.int32)
    flags = (owner_ids[:, None] == my_owners[None, :]).astype(jnp.int32)
    counts = running_count(flags)
    position = jnp.sum(flags * counts, axis=0) - 1
    flat = my_owners * capacity + position
    choose = (flat[:, None] == jnp.arange(devices * capacity, dtype=jnp.int32)[None, :]).astype(bf16)
    pieces = fronts(selector.reshape(n_row, -1, local_rows), parent_solution, choose,
                    border_tile[0], pivot_inverse[0], pivot_rhs[0])
    return jnp.sum(pieces, axis=0)[None]


def solution(mesh):
    return jax.shard_map(
        shards,
        mesh=mesh,
        in_specs=(
            P(("child", "row", "col"), None),
            P(),
            P(),
            P("child", "row", "col"),
            P("child", "row", "col"),
            P("child", "col", None),
        ),
        out_specs=P("child", ("row", "col"), None),
        check_vma=False,
    )
```

```python
import functools
import jax
import jax.numpy as jnp
from jax import lax
from jax.experimental import pallas as pl
from jax.experimental.pallas import tpu as pltpu
from jax.sharding import PartitionSpec as P

PIECE = 128
SLOTS = 4
SLACK = 3
SKEW = 2
bf16, f32 = jnp.bfloat16, jnp.float32


def split2(x):
    hi = x.astype(bf16)
    return hi, (x - hi.astype(f32)).astype(bf16)


def front_kernel(n_child, n_row, n_col, sel_ref, parent_ref, choose_ref, tile_ref, inv_ref, rhs_ref, out_ref,
                 picked, received, bv_own, bv_all, b_hi, b_lo, tbuf, ibuf, rhs, part, up_s, up_r, dn_s, dn_r, red, acc,
                 g_send, g_recv, tile_sem, inv_sem, rhs_sem, bv_send, bv_recv, us_sem, ur_sem, ds_sem, dr_sem,
                 c_send, c_recv, own_sem):
    row = lax.axis_index("row")
    col = lax.axis_index("col")
    last = n_row - 1
    n_sub = part.shape[0]
    block = bv_own.shape[0]
    child = lax.axis_index("child")
    devices = n_child * n_row * n_col
    me = (child * n_row + row) * n_col + col
    cap = picked.shape[0] // devices
    out_rows = acc.shape[0] // n_col
    lead = SKEW * last + SLACK
    rb = min(512, out_rows)
    n_rb = acc.shape[0] // rb
    per = out_rows // rb

    def tile_copy(j):
        return pltpu.make_async_copy(
            tile_ref.at[:, pl.ds(pl.multiple_of(j * PIECE, PIECE), PIECE)], tbuf.at[j], tile_sem.at[j])

    def inv_copy(j):
        slot = lax.rem(j, SLOTS)
        return pltpu.make_async_copy(
            inv_ref.at[:, pl.ds(pl.multiple_of(j * PIECE, PIECE), PIECE)], ibuf.at[slot], inv_sem.at[slot])

    rhs_copy = pltpu.make_async_copy(rhs_ref, rhs, rhs_sem)

    def up_copy(j):
        return pltpu.make_async_remote_copy(
            src_ref=up_s.at[j], dst_ref=up_r.at[j], send_sem=us_sem.at[j], recv_sem=ur_sem.at[j],
            device_id={"row": row + 1}, device_id_type=pl.DeviceIdType.MESH)

    def dn_copy(j):
        return pltpu.make_async_remote_copy(
            src_ref=dn_s.at[j], dst_ref=dn_r.at[j], send_sem=ds_sem.at[j], recv_sem=dr_sem.at[j],
            device_id={"row": row - 1}, device_id_type=pl.DeviceIdType.MESH)

    def start_tile(j, c):
        tile_copy(j).start()
        return c


    barrier = pltpu.get_barrier_semaphore()

    def coords(d):
        t = lax.rem(me + d, devices)
        return (t // (n_row * n_col), lax.rem(t // n_col, n_row), lax.rem(t, n_col))

    def greet(d, c):
        pl.semaphore_signal(barrier, inc=1, device_id=coords(d), device_id_type=pl.DeviceIdType.MESH)
        return c

    lax.fori_loop(1, devices, greet, 0)
    p_hi, p_lo = split2(parent_ref[...])
    picked[...] = (jnp.dot(sel_ref[...], p_hi, preferred_element_type=f32)
                   + jnp.dot(sel_ref[...], p_lo, preferred_element_type=f32))
    pl.semaphore_wait(barrier, devices - 1)

    def give(d):
        t = lax.rem(me + d, devices)
        return pltpu.make_async_remote_copy(
            src_ref=picked.at[pl.ds(pl.multiple_of(t * cap, 8), cap), :],
            dst_ref=received.at[pl.ds(pl.multiple_of(me * cap, 8), cap), :],
            send_sem=g_send.at[d], recv_sem=g_recv.at[d],
            device_id=coords(d), device_id_type=pl.DeviceIdType.MESH)

    def start_give(d, c):
        give(d).start()
        return c

    def end_give(d, c):
        give(d).wait_recv()
        return c

    lax.fori_loop(1, devices, start_give, 0)
    lax.fori_loop(0, n_sub, start_tile, 0)
    rhs_copy.start()
    for j in range(min(SLOTS, n_sub)):
        inv_copy(j).start()
    mine = pl.ds(pl.multiple_of(me * cap, 8), cap)
    received[mine, :] = picked[mine, :]
    acc[...] = jnp.zeros_like(acc)
    lax.fori_loop(1, devices, end_give, 0)
    g_hi, g_lo = split2(received[...])
    bv_own[...] = (jnp.dot(choose_ref[...], g_hi, preferred_element_type=f32)
                   + jnp.dot(choose_ref[...], g_lo, preferred_element_type=f32))

    bv_copies = []
    for q in range(n_col - 1):
        copy = pltpu.make_async_remote_copy(
            src_ref=bv_own, dst_ref=bv_all.at[q], send_sem=bv_send.at[q], recv_sem=bv_recv.at[q],
            device_id={"col": lax.rem(col + 1 + q, n_col)}, device_id_type=pl.DeviceIdType.MESH)
        copy.start()
        bv_copies.append(copy)

    def place(owner, value):
        rows = pl.ds(pl.multiple_of(owner * block, block), block)
        hi, lo = split2(value)
        b_hi[rows, :] = hi
        b_lo[rows, :] = lo

    place(col, bv_own[...])
    for q in range(n_col - 1):
        bv_copies[q].wait_recv()
        place(lax.rem(col + n_col - 1 - q, n_col), bv_all[q])

    def compute_part(j):
        tile_copy(j).wait()
        hi, lo = split2(tbuf[j])
        dims = (((0,), (0,)), ((), ()))
        out = lax.dot_general(hi, b_hi[...], dims, preferred_element_type=f32)
        out += lax.dot_general(hi, b_lo[...], dims, preferred_element_type=f32)
        out += lax.dot_general(lo, b_hi[...], dims, preferred_element_type=f32)
        part[j] = out

    def stage_up(j):
        @pl.when(row == 0)
        def _():
            up_s[j] = part[j]

        @pl.when(row > 0)
        def _():
            up_copy(j).wait_recv()
            up_s[j] = part[j] + up_r[j]

        @pl.when(row < last)
        def _():
            up_copy(j).start()

    def stage_down(j):
        @pl.when(row < last)
        def _():
            dn_copy(j).wait_recv()

        @pl.when(row == last)
        def _():
            dn_s[j] = part[j]

        @pl.when((row > 0) & (row < last))
        def _():
            dn_s[j] = part[j] + dn_r[j]

        @pl.when(row > 0)
        def _():
            dn_copy(j).start()

    def reduce_piece(j):
        @pl.when(row < last)
        def _():
            red[...] = rhs[pl.ds(pl.multiple_of(j * PIECE, PIECE), PIECE), :] - (up_s[j] + dn_r[j])

        @pl.when(row == last)
        def _():
            red[...] = rhs[pl.ds(pl.multiple_of(j * PIECE, PIECE), PIECE), :] - up_s[j]

        r_hi, r_lo = split2(red[...])
        inv_copy(j).wait()
        return jnp.concatenate([r_hi, r_lo, r_hi], axis=0)

    def add_rows(slot, b, right):
        rows = pl.ds(pl.multiple_of(b * rb, rb), rb)
        hi, lo = split2(ibuf[slot, rows, :])
        left = jnp.concatenate([hi, hi, lo], axis=1)
        acc[rows, :] += jnp.dot(left, right, preferred_element_type=f32)

    def step(s, c):
        @pl.when(s < n_sub)
        def _():
            compute_part(s)

        up_lag = jnp.where(row == last, lead, SKEW * row)
        dn_lag = jnp.where(row == 0, lead, SKEW * (last - row))
        ju = s - up_lag
        jd = s - dn_lag

        @pl.when((ju >= 0) & (ju < n_sub))
        def _():
            stage_up(ju)

        @pl.when((jd >= 0) & (jd < n_sub))
        def _():
            stage_down(jd)

        lag = jnp.maximum(up_lag, dn_lag)

        @pl.when(s == lag)
        def _():
            rhs_copy.wait()

        jf = s - lag

        @pl.when((jf >= 0) & (jf < n_sub - 1))
        def _():
            slot = lax.rem(jf, SLOTS)
            right = reduce_piece(jf)
            for b in range(n_rb):
                add_rows(slot, b, right)

            @pl.when(jf + SLOTS < n_sub)
            def _():
                inv_copy(jf + SLOTS).start()

        return c

    lax.fori_loop(0, n_sub + lead, step, 0)

    right = reduce_piece(n_sub - 1)
    slot = (n_sub - 1) % SLOTS
    sends = []
    for q in range(n_col):
        owner = lax.rem(col + 1 + q, n_col)
        for i in range(per):
            b = owner * per + i
            add_rows(slot, b, right)
            src = acc.at[pl.ds(pl.multiple_of(b * rb, rb), rb), :]
            dst = out_ref.at[col, pl.ds(i * rb, rb), :]
            if q < n_col - 1:
                copy = pltpu.make_async_remote_copy(
                    src_ref=src, dst_ref=dst, send_sem=c_send.at[q, i], recv_sem=c_recv.at[q, i],
                    device_id={"col": owner}, device_id_type=pl.DeviceIdType.MESH)
            else:
                copy = pltpu.make_async_copy(src, dst, own_sem.at[i])
            copy.start()
            sends.append(copy)
    for copy in bv_copies:
        copy.wait_send()

    def drain(j, c):
        @pl.when(row < last)
        def _():
            up_copy(j).wait_send()

        @pl.when(row > 0)
        def _():
            dn_copy(j).wait_send()

        return c

    lax.fori_loop(0, n_sub, drain, 0)

    def end_send(d, c):
        give(d).wait_send()
        return c

    lax.fori_loop(1, devices, end_send, 0)
    for copy in sends:
        copy.wait()


def fronts(selector, parent, choose, tile, inverse, rhs):
    n_child = lax.axis_size("child")
    n_row = lax.axis_size("row")
    n_col = lax.axis_size("col")
    block, wide = choose.shape
    loads = parent.shape[1]
    devices = n_child * n_row * n_col
    border, pivots = tile.shape
    rows = inverse.shape[0]
    n_sub = pivots // PIECE
    out_rows = rows // n_col
    per = out_rows // min(512, out_rows)
    dma = pltpu.SemaphoreType.DMA
    stream = pltpu.VMEM((n_sub, PIECE, loads), f32)
    hbm = pl.BlockSpec(memory_space=pl.ANY)
    return pl.pallas_call(
        functools.partial(front_kernel, n_child, n_row, n_col),
        out_shape=jax.ShapeDtypeStruct((n_col, out_rows, loads), f32),
        in_specs=[pl.BlockSpec(memory_space=pltpu.VMEM)] * 3 + [hbm] * 3,
        out_specs=hbm,
        scratch_shapes=[
            pltpu.VMEM((wide, loads), f32),
            pltpu.VMEM((wide, loads), f32),
            pltpu.VMEM((block, loads), f32),
            pltpu.VMEM((max(n_col - 1, 1), block, loads), f32),
            pltpu.VMEM((border, loads), bf16),
            pltpu.VMEM((border, loads), bf16),
            pltpu.VMEM((n_sub, border, PIECE), f32),
            pltpu.VMEM((SLOTS, rows, PIECE), f32),
            pltpu.VMEM((pivots, loads), f32),
            stream, stream, stream, stream, stream,
            pltpu.VMEM((PIECE, loads), f32),
            pltpu.VMEM((rows, loads), f32),
            dma((devices,)), dma((devices,)),
            dma((n_sub,)), dma((SLOTS,)), dma(()),
            dma((n_col,)), dma((n_col,)),
            dma((n_sub,)), dma((n_sub,)), dma((n_sub,)), dma((n_sub,)),
            dma((n_col, per)), dma((n_col, per)), dma((per,)),
        ],
        compiler_params=pltpu.CompilerParams(
            collective_id=0, has_side_effects=True, vmem_limit_bytes=60 * 1024 * 1024),
    )(selector, parent, choose, tile, inverse, rhs)


def running_count(flags):
    length = flags.shape[1]
    steps = jnp.arange(length, dtype=jnp.int32)
    upper = (steps[:, None] <= steps[None, :]).astype(jnp.bfloat16)
    counted = jnp.dot(flags.astype(jnp.bfloat16), upper, preferred_element_type=jnp.float32)
    return counted.astype(jnp.int32)


def shards(parent_solution, border_owner, border_slot, border_tile, pivot_inverse, pivot_rhs):
    devices = lax.axis_size(("child", "row", "col"))
    my_index = lax.axis_index(("child", "row", "col"))
    n_row = lax.axis_size("row")
    n_col = lax.axis_size("col")
    owners = border_owner[:, :, 0]
    border_rows = owners.shape[1]
    block_rows = border_rows // (n_row * n_col)
    capacity = -(-2 * ((block_rows + devices - 1) // devices) // 8) * 8
    local_rows = parent_solution.shape[0]
    request_owner = owners.reshape(devices, block_rows)
    request_slot = border_slot.reshape(devices, block_rows)
    matched = (request_owner == my_index).astype(jnp.int32)
    position = running_count(matched) - 1
    places = jnp.arange(capacity, dtype=jnp.int32)
    hit = (matched[:, None, :] == 1) & (position[:, None, :] == places[None, :, None])
    table = jnp.sum(jnp.where(hit, request_slot[:, None, :], 0), axis=2)
    filled = jnp.any(hit, axis=2)
    rows_idx = jnp.arange(local_rows, dtype=jnp.int32)
    selector = ((table[:, :, None] == rows_idx[None, None, :]) & filled[:, :, None]).astype(bf16)
    my_owners = lax.dynamic_index_in_dim(request_owner, my_index, 0, keepdims=False)
    owner_ids = jnp.arange(devices, dtype=jnp.int32)
    flags = (owner_ids[:, None] == my_owners[None, :]).astype(jnp.int32)
    counts = running_count(flags)
    position = jnp.sum(flags * counts, axis=0) - 1
    flat = my_owners * capacity + position
    choose = (flat[:, None] == jnp.arange(devices * capacity, dtype=jnp.int32)[None, :]).astype(bf16)
    pieces = fronts(selector.reshape(-1, local_rows), parent_solution, choose,
                    border_tile[0], pivot_inverse[0], pivot_rhs[0])
    return jnp.sum(pieces, axis=0)[None]


def solution(mesh):
    return jax.shard_map(
        shards,
        mesh=mesh,
        in_specs=(
            P(("child", "row", "col"), None),
            P(),
            P(),
            P("child", "row", "col"),
            P("child", "row", "col"),
            P("child", "col", None),
        ),
        out_specs=P("child", ("row", "col"), None),
        check_vma=False,
    )
```
